32 devices in a mesh: wide: 4 (over z), narrow: 8 (over y, x, core).
Axes of the slice: x: 2, y: 2, z: 4, core: 2. Of those that a mesh axis runs over, the one named last changes fastest.
Arguments:
- samples: bfloat16 [1024, 2, 102144], P(('wide', 'narrow')), may hold values from -6 to 6
- filter_taps: float32 [16, 256], replicated, may hold values from -1.5 to 1.5
- beam_weights: bfloat16 [256, 2, 2, 512, 1024], P(('narrow', 'wide')), may hold values from -0.1875 to 0.1875
- smooth_kernel: float32 [33, 33], replicated, may hold values from -0.1875 to 0.1875
Outputs:
- detection: float32 [256, 48, 1024], P('narrow', None, 'wide')
The draws below stay inside these ranges and needn't reach their ends.
All inputs are finite; a program needn't handle non-finite values.
Results may differ from the reference program's by a relative error of at most 0.012.
The reference program's roundings to bfloat16 on the way count: a program that leaves them out, or rounds other values in their place, can miss the bound.
Values may be sent and summed in bfloat16 or wider, within the bound.
A program may use at most 320 MiB of HBM per device.

```python
import jax
import jax.numpy as jnp
from jax import lax

DISHES = 512
POLS = 2
NFFT = 256
TAPS = 16
BEAMS = 1024
INTEG = 8
HALF = 16
SPECTRA = 384
INPUTS = 1024
CHANNELS = 256
TBINS = 48
SAMPLES = 102144


def levels(stream_key, dims, split, smallest, high):
    def one(axis_at, blocks):
        steps = jax.random.uniform(jax.random.fold_in(jax.random.fold_in(stream_key, 6), axis_at), (blocks,), jnp.float32, smallest / len(split), high / len(split))
        return jnp.repeat(jnp.exp(steps), dims[axis_at] // blocks).reshape((-1,) + (1,) * (len(dims) - axis_at - 1))

    gain = one(*split[0])
    for cut in split[1:]:
        gain = gain * one(*cut)
    return gain


def bell_draw(stream_key, shape, spread, reach, shards=(), kind=jnp.bfloat16):
    array = jax.random.normal(stream_key, shape, jnp.float32) * spread
    if len(shards) > 0:
        array = levels(stream_key, shape, shards, -0.22, 0.18) * array
    return jnp.clip(array, min=-reach, max=reach).astype(kind)


def setup_inputs(seed: int = 0) -> dict:
    arg_keys = jax.random.split(jax.random.key(seed), 5)
    return {
        "samples": bell_draw(arg_keys[0], (INPUTS, 2, SAMPLES), 1.0, 6.0, ((0, 32),)),
        "filter_taps": bell_draw(arg_keys[1], (TAPS, NFFT), TAPS ** -0.5, 1.5, (), jnp.float32),
        "beam_weights": bell_draw(arg_keys[2], (CHANNELS, POLS, 2, DISHES, BEAMS), (2 * DISHES) ** -0.5, 0.1875, ((0, 32),)),
        "smooth_kernel": bell_draw(arg_keys[3], (2 * HALF + 1, 2 * HALF + 1), ((2 * HALF + 1) * (2 * HALF + 1)) ** -0.5, 0.1875, (), jnp.float32),
    }


def fourier_rows(points):
    column = jnp.arange(points, dtype=jnp.int32)
    phase_index = (column[:, None] * column[None, :]) % points
    angles = phase_index.astype(jnp.float32) * jnp.float32(2.0 * jnp.pi / points)
    scale = jnp.float32(1.0 / (points ** 0.5))
    cosine = jnp.cos(angles) * scale
    sine_part = jnp.sin(angles) * scale
    real_row = jnp.stack([cosine, sine_part], axis=1)
    imag_row = jnp.stack([-sine_part, cosine], axis=1)
    return jnp.stack([real_row, imag_row], axis=1).reshape(2 * points, 2, points)


def channelize_one(signal_in, filter_taps, fourier_table):
    tap_count, points = filter_taps.shape
    frames = signal_in.shape[1] // points
    spectra = frames - tap_count + 1
    signal = signal_in.astype(jnp.float32).reshape(2, frames, points)
    windowed = filter_taps[0] * signal[:, 0:spectra]
    for tap_index in range(1, tap_count):
        windowed = windowed + filter_taps[tap_index] * signal[:, tap_index:tap_index + spectra]
    spectrum = jnp.einsum("pab,asb->ps", fourier_table, windowed, precision=lax.Precision.HIGH)
    return spectrum.astype(jnp.bfloat16).reshape(points, 2, spectra)


def channel_power(voltage, weights):
    values = voltage.astype(jnp.float32).reshape(POLS, DISHES, 2, SPECTRA)
    coeffs = weights.astype(jnp.float32)
    real_in = values[:, :, 0]
    imag_in = values[:, :, 1]
    real_w = coeffs[:, 0]
    imag_w = coeffs[:, 1]
    real_out = jnp.einsum("pds,pdb->psb", real_in, real_w) - jnp.einsum("pds,pdb->psb", imag_in, imag_w)
    imag_out = jnp.einsum("pds,pdb->psb", real_in, imag_w) + jnp.einsum("pds,pdb->psb", imag_in, real_w)
    energy = jnp.sum(real_out * real_out + imag_out * imag_out, axis=0)
    binned = energy.reshape(TBINS, INTEG, BEAMS).sum(axis=1)
    return (binned / jnp.float32(POLS * INTEG)).astype(jnp.bfloat16)


def reference(samples, filter_taps, beam_weights, smooth_kernel):
    fourier_table = fourier_rows(NFFT)

    def channelize_input(signal_in):
        return channelize_one(signal_in, filter_taps, fourier_table)

    voltage = lax.map(channelize_input, samples)
    by_channel = jnp.transpose(voltage, (1, 0, 2, 3))

    def power_of(paired):
        return channel_power(paired[0], paired[1])

    intensity = lax.map(power_of, (by_channel, beam_weights))
    values = intensity.astype(jnp.float32)
    centered = values - jnp.mean(values, axis=1, keepdims=True)
    image = jnp.transpose(centered, (2, 0, 1))[:, None]
    kernel = smooth_kernel[None, None]
    filtered = lax.conv_general_dilated(image, kernel, (1, 1), [(HALF, HALF), (HALF, HALF)], precision=lax.Precision.HIGH)
    return jnp.transpose(filtered[:, 0], (1, 2, 0))
```

```python
import functools

import jax
import jax.numpy as jnp
from jax import lax
from jax.experimental import pallas as pl
from jax.experimental.pallas import tpu as pltpu
from jax.sharding import PartitionSpec as P

INTEG = 8
HALF = 16
LANES = 128
PORTION = 128
BAND = 8


def with_halo(block, sides, width):
    for axis, dim in sides:
        count = lax.axis_size(axis)
        forward = [(i, i + 1) for i in range(count - 1)]
        backward = [(target, source) for source, target in forward]
        low = lax.ppermute(
            lax.slice_in_dim(block, block.shape[dim] - width, None, axis=dim), axis, forward
        )
        high = lax.ppermute(lax.slice_in_dim(block, 0, width, axis=dim), axis, backward)
        block = jnp.concatenate([low, block, high], axis=dim)
    return block


def fourier_rows(points, owner_of):
    column = jnp.arange(points, dtype=jnp.int32)
    channel = owner_of(column)
    phase_index = channel[:, None] * column[None, :] % points
    angles = phase_index.astype(jnp.float32) * jnp.float32(2.0 * jnp.pi / points)
    scale = jnp.float32(1.0 / points**0.5)
    cosine = jnp.cos(angles) * scale
    sine_part = jnp.sin(angles) * scale
    real_row = jnp.stack([cosine, sine_part], axis=1)
    imag_row = jnp.stack([-sine_part, cosine], axis=1)
    return jnp.stack([real_row, imag_row], axis=1).reshape(2 * points, 2 * points)


def split(value):
    high = value.astype(jnp.bfloat16)
    return high, (value - high.astype(jnp.float32)).astype(jnp.bfloat16)


def channelize_kernel(
    taps_ref, table_ref, main_ref, halo_ref, out_ref, window_ref, high_ref, low_ref, turned_ref
):
    tap_count, points = taps_ref.shape
    group = main_ref.shape[1]
    spectra = main_ref.shape[2] // points
    high_ref[...], low_ref[...] = split(table_ref[...])
    blocks = spectra // tap_count

    for part in range(2):
        for tile in range(points // LANES):
            lane = tile * LANES
            column = part * (points // LANES) + tile
            for base in range(0, group, 8):
                coeffs = [
                    jnp.broadcast_to(taps_ref[tap : tap + 1, lane : lane + LANES], (8, LANES))
                    for tap in range(tap_count)
                ]

                def load(ref, frame):
                    start = pl.multiple_of(frame * points + lane, LANES)
                    rows = ref[part, base : base + 8, pl.ds(start, LANES)]
                    return rows.astype(jnp.float32)

                def emit(block, older, newer_ref, newer_base):
                    sums = list(older)
                    nexts = [None] * tap_count
                    for step in range(tap_count):
                        value = load(newer_ref, newer_base + step)
                        for index in range(tap_count):
                            tap = tap_count + step - index
                            if tap < tap_count:
                                sums[index] = sums[index] + coeffs[tap] * value
                            tap = step - index
                            if 0 <= tap:
                                term = coeffs[tap] * value
                                nexts[index] = (
                                    term if nexts[index] is None else nexts[index] + term
                                )
                        window_ref[
                            column,
                            pl.ds(base * spectra + block * tap_count + step, 8, stride=spectra),
                            :,
                        ] = sums[step]
                    return tuple(nexts)

                first = [None] * tap_count
                for step in range(tap_count):
                    value = load(main_ref, step)
                    for index in range(step + 1):
                        term = coeffs[step - index] * value
                        first[index] = term if first[index] is None else first[index] + term

                def body(block, older):
                    return emit(block, older, main_ref, (block + 1) * tap_count)

                older = lax.fori_loop(0, blocks - 1, body, tuple(first))
                sums = list(older)
                window_ref[
                    column,
                    pl.ds(base * spectra + (blocks - 1) * tap_count, 8, stride=spectra),
                    :,
                ] = sums[0]
                for step in range(tap_count - 1):
                    value = load(halo_ref, step)
                    for index in range(step + 1, tap_count):
                        sums[index] = sums[index] + coeffs[tap_count + step - index] * value
                    window_ref[
                        column,
                        pl.ds(
                            base * spectra + (blocks - 1) * tap_count + step + 1, 8, stride=spectra
                        ),
                        :,
                    ] = sums[step + 1]

    columns = window_ref.shape[0]
    contract = (((1,), (1,)), ((), ()))

    @pl.loop(0, group)
    def _(index):
        rows = pl.ds(pl.multiple_of(index * spectra, spectra), spectra)
        signal = jnp.concatenate([window_ref[column, rows, :] for column in range(columns)], axis=1)
        high, low = split(signal)
        product = functools.partial(
            lax.dot_general, dimension_numbers=contract, preferred_element_type=jnp.float32
        )
        result = (
            product(low_ref[...], high) + product(high_ref[...], low) + product(high_ref[...], high)
        )
        turned_ref[pl.ds(index, result.shape[0], stride=group), :] = result

    out_ref[...] = turned_ref[...].reshape(out_ref.shape).astype(out_ref.dtype)


def channelize(by_part, filter_taps, table, portion):
    tap_count, points = filter_taps.shape
    inputs_here = by_part.shape[1]
    group = min(16, inputs_here)
    rows = table.shape[0]
    halo = tap_count * points
    return pl.pallas_call(
        channelize_kernel,
        grid=(inputs_here // group,),
        in_specs=[
            pl.BlockSpec(filter_taps.shape, lambda g: (0, 0)),
            pl.BlockSpec(table.shape, lambda g: (0, 0)),
            pl.BlockSpec((2, group, PORTION * points), lambda g: (0, g, portion)),
            pl.BlockSpec(
                (2, group, halo), lambda g: (0, g, (portion + 1) * (PORTION // tap_count))
            ),
        ],
        out_specs=pl.BlockSpec((rows, group, PORTION), lambda g: (0, g, 0)),
        out_shape=jax.ShapeDtypeStruct((rows, inputs_here, PORTION), jnp.bfloat16),
        scratch_shapes=[
            pltpu.VMEM((2 * points // LANES, group * PORTION, LANES), jnp.float32),
            pltpu.VMEM(table.shape, jnp.bfloat16),
            pltpu.VMEM(table.shape, jnp.bfloat16),
            pltpu.VMEM((rows * group, PORTION), jnp.float32),
        ],
        cost_estimate=pl.CostEstimate(
            flops=6 * rows * rows * inputs_here * PORTION,
            bytes_accessed=8 * inputs_here * points * PORTION,
            transcendentals=0,
        ),
        compiler_params=pltpu.CompilerParams(vmem_limit_bytes=48 * 1024 * 1024),
        name=f"channelize_{portion}",
    )(filter_taps, table, by_part, by_part)


def beam_kernel(voltage_ref, weight_ref, out_ref):
    sources, _, inputs_each, spectra = voltage_ref.shape
    pols, _, dishes, beams = weight_ref.shape[1:]
    per_pol = sources // pols

    def dish_rows(pol, part):
        rows = voltage_ref[pol * per_pol : (pol + 1) * per_pol, part]
        if inputs_each % 16 != 0:
            rows = rows.astype(jnp.float32)
        return rows.reshape(dishes, spectra).astype(jnp.float32).T.astype(jnp.bfloat16)

    energy = None
    for pol in range(pols):
        real = dish_rows(pol, 0)
        imag = dish_rows(pol, 1)
        left = jnp.concatenate(
            [jnp.concatenate([real, -imag], axis=1), jnp.concatenate([imag, real], axis=1)], axis=0
        )
        weights = weight_ref[0, pol].reshape(2 * dishes, beams)
        formed = jnp.dot(left, weights, preferred_element_type=jnp.float32)
        squares = formed * formed
        power = squares[:spectra] + squares[spectra:]
        energy = power if energy is None else energy + power
    binned = energy.reshape(spectra // INTEG, INTEG, beams).sum(axis=1)
    out_ref[0] = (binned * jnp.float32(1.0 / (pols * INTEG))).astype(jnp.bfloat16)


def beam_power(turned, beam_weights, portion):
    sources, rows, inputs_each, spectra = turned.shape
    per_device, pols, _, dishes, beams = beam_weights.shape
    return pl.pallas_call(
        beam_kernel,
        grid=(per_device,),
        in_specs=[
            pl.BlockSpec((sources, 2, inputs_each, spectra), lambda c: (0, c, 0, 0)),
            pl.BlockSpec((1, pols, 2, dishes, beams), lambda c: (c, 0, 0, 0, 0)),
        ],
        out_specs=pl.BlockSpec((1, spectra // INTEG, beams), lambda c: (c, 0, 0)),
        out_shape=jax.ShapeDtypeStruct((per_device, spectra // INTEG, beams), jnp.bfloat16),
        cost_estimate=pl.CostEstimate(
            flops=16 * per_device * dishes * spectra * beams,
            bytes_accessed=2 * beam_weights.size + 2 * turned.size,
            transcendentals=0,
        ),
        compiler_params=pltpu.CompilerParams(vmem_limit_bytes=48 * 1024 * 1024),
        name=f"beams_{portion}",
    )(turned, beam_weights)


def band_matrix(smooth_kernel, bin_count):
    extent = smooth_kernel.shape[0]
    half_width = extent // 2
    span = BAND + extent - 1
    offsets = jnp.arange(extent, dtype=jnp.int32)
    bins = jnp.arange(bin_count, dtype=jnp.int32)
    distance = bins[None, :] - bins[:, None] + half_width
    in_time = (distance[None] == offsets[:, None, None]).astype(jnp.float32)
    steps = jnp.arange(span, dtype=jnp.int32)[None, :] - jnp.arange(BAND, dtype=jnp.int32)[:, None]
    in_band = (steps[None] == offsets[:, None, None]).astype(jnp.float32)
    rows = jnp.einsum("kcj,kd->cjd", in_band, smooth_kernel, precision=lax.Precision.HIGHEST)
    matrix = jnp.einsum("cjd,dtu->ctju", rows, in_time, precision=lax.Precision.HIGHEST)
    return matrix.reshape(BAND * bin_count, span * bin_count)


def smooth(extended, matrix, half_width):
    channels_here = extended.shape[0] - 2 * half_width
    bin_count, beams = extended.shape[1:]
    values = extended.astype(jnp.float32)
    centered = values - jnp.mean(values, axis=1, keepdims=True)
    flat = centered.reshape(-1, beams)
    pieces = []
    for start in range(0, channels_here, BAND):
        rows = lax.slice_in_dim(flat, start * bin_count, start * bin_count + matrix.shape[1], axis=0)
        pieces.append(
            jnp.dot(
                matrix, rows, precision=lax.Precision.HIGH, preferred_element_type=jnp.float32
            )
        )
    return jnp.concatenate(pieces, axis=0).reshape(channels_here, bin_count, beams)


def body(samples, filter_taps, beam_weights, smooth_kernel):
    tap_count, points = filter_taps.shape
    wide_count = lax.axis_size("wide")
    narrow_count = lax.axis_size("narrow")
    devices = wide_count * narrow_count
    per_device = points // devices

    def owner_of(column):
        device_slot = column // per_device
        return (
            device_slot % narrow_count * wide_count + device_slot // narrow_count
        ) * per_device + column % per_device

    table = fourier_rows(points, owner_of)
    frames = samples.shape[2] // points
    spectra = frames - tap_count + 1
    by_part = jnp.transpose(samples, (1, 0, 2))
    matrix = band_matrix(smooth_kernel, spectra // INTEG)
    turned = []
    for portion in range(spectra // PORTION):
        voltage = channelize(by_part, filter_taps, table, portion)
        arranged = voltage.reshape(devices, 2 * per_device, -1, PORTION)
        turned.append(
            lax.all_to_all(arranged, ("wide", "narrow"), split_axis=0, concat_axis=0, tiled=True)
        )
    pieces = [beam_power(block, beam_weights, portion) for portion, block in enumerate(turned)]
    intensity = jnp.concatenate(pieces, axis=1)
    by_beam = lax.all_to_all(intensity, "wide", split_axis=2, concat_axis=0, tiled=True)
    half_width = smooth_kernel.shape[0] // 2
    extended = with_halo(by_beam, (("narrow", 0),), half_width)
    return smooth(extended, matrix, half_width)


def solution(mesh):
    placed = (
        P(("wide", "narrow"), None, None),
        P(),
        P(("narrow", "wide"), None, None, None, None),
        P(),
    )
    return jax.shard_map(
        body, mesh=mesh, in_specs=placed, out_specs=P("narrow", None, "wide"), check_vma=False
    )
```

```python
import functools

import jax
import jax.numpy as jnp
from jax import lax
from jax.experimental import pallas as pl
from jax.experimental.pallas import tpu as pltpu
from jax.sharding import PartitionSpec as P

INTEG = 8
HALF = 16
LANES = 128
PORTION = 128
BAND = 8


def with_halo(block, sides, width):
    for axis, dim in sides:
        count = lax.axis_size(axis)
        forward = [(i, i + 1) for i in range(count - 1)]
        backward = [(target, source) for source, target in forward]
        low = lax.ppermute(
            lax.slice_in_dim(block, block.shape[dim] - width, None, axis=dim), axis, forward
        )
        high = lax.ppermute(lax.slice_in_dim(block, 0, width, axis=dim), axis, backward)
        block = jnp.concatenate([low, block, high], axis=dim)
    return block


def fourier_rows(points, owner_of):
    column = jnp.arange(points, dtype=jnp.int32)
    channel = owner_of(column)
    phase_index = channel[:, None] * column[None, :] % points
    angles = phase_index.astype(jnp.float32) * jnp.float32(2.0 * jnp.pi / points)
    scale = jnp.float32(1.0 / points**0.5)
    cosine = jnp.cos(angles) * scale
    sine_part = jnp.sin(angles) * scale
    real_row = jnp.stack([cosine, sine_part], axis=1)
    imag_row = jnp.stack([-sine_part, cosine], axis=1)
    return jnp.stack([real_row, imag_row], axis=1).reshape(2 * points, 2 * points)


def split(value):
    high = value.astype(jnp.bfloat16)
    return high, (value - high.astype(jnp.float32)).astype(jnp.bfloat16)


def channelize_kernel(
    taps_ref, table_ref, main_ref, halo_ref, out_ref, window_ref, high_ref, low_ref, turned_ref
):
    tap_count, points = taps_ref.shape
    group = main_ref.shape[1]
    spectra = main_ref.shape[2] // points
    high_ref[...], low_ref[...] = split(table_ref[...])
    blocks = spectra // tap_count

    for part in range(2):
        for tile in range(points // LANES):
            lane = tile * LANES
            column = part * (points // LANES) + tile
            for base in range(0, group, 8):
                coeffs = [
                    jnp.broadcast_to(taps_ref[tap : tap + 1, lane : lane + LANES], (8, LANES))
                    for tap in range(tap_count)
                ]

                def load(ref, frame):
                    start = pl.multiple_of(frame * points + lane, LANES)
                    rows = ref[part, base : base + 8, pl.ds(start, LANES)]
                    return rows.astype(jnp.float32)

                def emit(block, older, newer_ref, newer_base):
                    sums = list(older)
                    nexts = [None] * tap_count
                    for step in range(tap_count):
                        value = load(newer_ref, newer_base + step)
                        for index in range(tap_count):
                            tap = tap_count + step - index
                            if tap < tap_count:
                                sums[index] = sums[index] + coeffs[tap] * value
                            tap = step - index
                            if 0 <= tap:
                                term = coeffs[tap] * value
                                nexts[index] = (
                                    term if nexts[index] is None else nexts[index] + term
                                )
                        window_ref[
                            column,
                            pl.ds(base * spectra + block * tap_count + step, 8, stride=spectra),
                            :,
                        ] = sums[step]
                    return tuple(nexts)

                first = [None] * tap_count
                for step in range(tap_count):
                    value = load(main_ref, step)
                    for index in range(step + 1):
                        term = coeffs[step - index] * value
                        first[index] = term if first[index] is None else first[index] + term

                def body(block, older):
                    return emit(block, older, main_ref, (block + 1) * tap_count)

                older = lax.fori_loop(0, blocks - 1, body, tuple(first))
                sums = list(older)
                window_ref[
                    column,
                    pl.ds(base * spectra + (blocks - 1) * tap_count, 8, stride=spectra),
                    :,
                ] = sums[0]
                for step in range(tap_count - 1):
                    value = load(halo_ref, step)
                    for index in range(step + 1, tap_count):
                        sums[index] = sums[index] + coeffs[tap_count + step - index] * value
                    window_ref[
                        column,
                        pl.ds(
                            base * spectra + (blocks - 1) * tap_count + step + 1, 8, stride=spectra
                        ),
                        :,
                    ] = sums[step + 1]

    columns = window_ref.shape[0]
    contract = (((1,), (1,)), ((), ()))

    @pl.loop(0, group)
    def _(index):
        rows = pl.ds(pl.multiple_of(index * spectra, spectra), spectra)
        signal = jnp.concatenate([window_ref[column, rows, :] for column in range(columns)], axis=1)
        high, low = split(signal)
        product = functools.partial(
            lax.dot_general, dimension_numbers=contract, preferred_element_type=jnp.float32
        )
        result = (
            product(low_ref[...], high) + product(high_ref[...], low) + product(high_ref[...], high)
        )
        turned_ref[pl.ds(index, result.shape[0], stride=group), :] = result

    out_ref[...] = turned_ref[...].reshape(out_ref.shape).astype(out_ref.dtype)


def channelize(by_part, filter_taps, table, portion):
    tap_count, points = filter_taps.shape
    inputs_here = by_part.shape[1]
    group = min(16, inputs_here)
    rows = table.shape[0]
    halo = tap_count * points
    return pl.pallas_call(
        channelize_kernel,
        grid=(inputs_here // group,),
        in_specs=[
            pl.BlockSpec(filter_taps.shape, lambda g: (0, 0)),
            pl.BlockSpec(table.shape, lambda g: (0, 0)),
            pl.BlockSpec((2, group, PORTION * points), lambda g: (0, g, portion)),
            pl.BlockSpec(
                (2, group, halo), lambda g: (0, g, (portion + 1) * (PORTION // tap_count))
            ),
        ],
        out_specs=pl.BlockSpec((rows, group, PORTION), lambda g: (0, g, 0)),
        out_shape=jax.ShapeDtypeStruct((rows, inputs_here, PORTION), jnp.bfloat16),
        scratch_shapes=[
            pltpu.VMEM((2 * points // LANES, group * PORTION, LANES), jnp.float32),
            pltpu.VMEM(table.shape, jnp.bfloat16),
            pltpu.VMEM(table.shape, jnp.bfloat16),
            pltpu.VMEM((rows * group, PORTION), jnp.float32),
        ],
        cost_estimate=pl.CostEstimate(
            flops=6 * rows * rows * inputs_here * PORTION,
            bytes_accessed=8 * inputs_here * points * PORTION,
            transcendentals=0,
        ),
        compiler_params=pltpu.CompilerParams(vmem_limit_bytes=48 * 1024 * 1024),
        name=f"channelize_{portion}",
    )(filter_taps, table, by_part, by_part)


def beam_kernel(voltage_ref, weight_ref, out_ref):
    sources, _, inputs_each, spectra = voltage_ref.shape
    pols, _, dishes, beams = weight_ref.shape[1:]
    per_pol = sources // pols

    def dish_rows(pol, part):
        rows = voltage_ref[pol * per_pol : (pol + 1) * per_pol, part]
        if inputs_each % 16 != 0:
            rows = rows.astype(jnp.float32)
        return rows.reshape(dishes, spectra).astype(jnp.float32).T.astype(jnp.bfloat16)

    energy = None
    for pol in range(pols):
        real = dish_rows(pol, 0)
        imag = dish_rows(pol, 1)
        left = jnp.concatenate(
            [jnp.concatenate([real, -imag], axis=1), jnp.concatenate([imag, real], axis=1)], axis=0
        )
        weights = weight_ref[0, pol].reshape(2 * dishes, beams)
        formed = jnp.dot(left, weights, preferred_element_type=jnp.float32)
        squares = formed * formed
        power = squares[:spectra] + squares[spectra:]
        energy = power if energy is None else energy + power
    binned = energy.reshape(spectra // INTEG, INTEG, beams).sum(axis=1)
    intensity = (binned * jnp.float32(1.0 / (pols * INTEG))).astype(jnp.bfloat16)
    share = out_ref.shape[3]
    for owner in range(out_ref.shape[0]):
        out_ref[owner, 0] = intensity[:, owner * share : (owner + 1) * share]


def beam_power(turned, beam_weights, portion, owners):
    sources, rows, inputs_each, spectra = turned.shape
    per_device, pols, _, dishes, beams = beam_weights.shape
    return pl.pallas_call(
        beam_kernel,
        grid=(per_device,),
        in_specs=[
            pl.BlockSpec((sources, 2, inputs_each, spectra), lambda c: (0, c, 0, 0)),
            pl.BlockSpec((1, pols, 2, dishes, beams), lambda c: (c, 0, 0, 0, 0)),
        ],
        out_specs=pl.BlockSpec(
            (owners, 1, spectra // INTEG, beams // owners), lambda c: (0, c, 0, 0)
        ),
        out_shape=jax.ShapeDtypeStruct(
            (owners, per_device, spectra // INTEG, beams // owners), jnp.bfloat16
        ),
        cost_estimate=pl.CostEstimate(
            flops=16 * per_device * dishes * spectra * beams,
            bytes_accessed=2 * beam_weights.size + 2 * turned.size,
            transcendentals=0,
        ),
        compiler_params=pltpu.CompilerParams(vmem_limit_bytes=48 * 1024 * 1024),
        name=f"beams_{portion}",
    )(turned, beam_weights)


def band_matrix(smooth_kernel, bin_count):
    extent = smooth_kernel.shape[0]
    half_width = extent // 2
    span = BAND + extent - 1
    offsets = jnp.arange(extent, dtype=jnp.int32)
    bins = jnp.arange(bin_count, dtype=jnp.int32)
    distance = bins[None, :] - bins[:, None] + half_width
    in_time = (distance[None] == offsets[:, None, None]).astype(jnp.float32)
    steps = jnp.arange(span, dtype=jnp.int32)[None, :] - jnp.arange(BAND, dtype=jnp.int32)[:, None]
    in_band = (steps[None] == offsets[:, None, None]).astype(jnp.float32)
    rows = jnp.einsum("kcj,kd->cjd", in_band, smooth_kernel, precision=lax.Precision.HIGHEST)
    matrix = jnp.einsum("cjd,dtu->ctju", rows, in_time, precision=lax.Precision.HIGHEST)
    return matrix.reshape(BAND * bin_count, span * bin_count)


def smooth(extended, matrix, half_width):
    channels_here = extended.shape[0] - 2 * half_width
    bin_count, beams = extended.shape[1:]
    values = extended.astype(jnp.float32)
    centered = values - jnp.mean(values, axis=1, keepdims=True)
    flat = centered.reshape(-1, beams)
    pieces = []
    for start in range(0, channels_here, BAND):
        rows = lax.slice_in_dim(flat, start * bin_count, start * bin_count + matrix.shape[1], axis=0)
        pieces.append(
            jnp.dot(
                matrix, rows, precision=lax.Precision.HIGH, preferred_element_type=jnp.float32
            )
        )
    return jnp.concatenate(pieces, axis=0).reshape(channels_here, bin_count, beams)


def body(samples, filter_taps, beam_weights, smooth_kernel):
    tap_count, points = filter_taps.shape
    wide_count = lax.axis_size("wide")
    narrow_count = lax.axis_size("narrow")
    devices = wide_count * narrow_count
    per_device = points // devices

    def owner_of(column):
        device_slot = column // per_device
        return (
            device_slot % narrow_count * wide_count + device_slot // narrow_count
        ) * per_device + column % per_device

    table = fourier_rows(points, owner_of)
    frames = samples.shape[2] // points
    spectra = frames - tap_count + 1
    by_part = jnp.transpose(samples, (1, 0, 2))
    matrix = band_matrix(smooth_kernel, spectra // INTEG)
    turned = []
    for portion in range(spectra // PORTION):
        voltage = channelize(by_part, filter_taps, table, portion)
        arranged = voltage.reshape(devices, 2 * per_device, -1, PORTION)
        turned.append(
            lax.all_to_all(arranged, ("wide", "narrow"), split_axis=0, concat_axis=0, tiled=True)
        )
    pieces = [
        beam_power(block, beam_weights, portion, wide_count)
        for portion, block in enumerate(turned)
    ]
    intensity = jnp.concatenate(pieces, axis=2)
    by_beam = lax.all_to_all(intensity, "wide", split_axis=0, concat_axis=0, tiled=True)
    by_beam = by_beam.reshape(-1, *by_beam.shape[2:])
    half_width = smooth_kernel.shape[0] // 2
    extended = with_halo(by_beam, (("narrow", 0),), half_width)
    return smooth(extended, matrix, half_width)


def solution(mesh):
    placed = (
        P(("wide", "narrow"), None, None),
        P(),
        P(("narrow", "wide"), None, None, None, None),
        P(),
    )
    return jax.shard_map(
        body, mesh=mesh, in_specs=placed, out_specs=P("narrow", None, "wide"), check_vma=False
    )
```
